256 devices in a mesh: img: 32 (over z_lo, x, y), pix: 8 (over z_hi, core).
Axes of the slice: x: 4, y: 4, z: 8 (z_hi: 4, z_lo: 2; z = z_hi * 2 + z_lo), core: 2. Of those that a mesh axis runs over, the one named last changes fastest.
Arguments:
- images: bfloat16 [8192, 16384], P('img', 'pix'), may hold values from -100 to 100
- references: bfloat16 [1536, 16384], P('img', 'pix'), may hold values from -6 to 6
- cycle_mask: int32 [16384], P('pix'), may hold values from 0 to 1, as said below
- view_class: int32 [1536], replicated, may hold values from 0 to 95, as said below
Outputs:
- view_sums: float32 [1536, 16384], P('img', 'pix')
- class_share: float32 [96], replicated
- image_evidence: float32 [8192], P(('img', 'pix'))
The draws below stay inside these ranges and needn't reach their ends.
Inputs may be any that keep to these rules, and one draw needn't show every extreme that they name: `cycle_mask`: only pixels whose distance from the image centre lies between an inner radius and 64 are 1; some of them are left out as defective, never those in even columns, so the cycle is never empty. `view_class`: every class is named by exactly 16 views.
All inputs are finite; a program needn't handle non-finite values.
Results may differ from the reference program's by a relative error of at most 0.0023.
Values may be sent and summed in bfloat16 or wider, within the bound.
No kernel may reach another device: no remote copies, remote signals or barrier semaphores. Data moves between devices by JAX's collectives and lax.ppermute only.
A program may use at most 64 MiB of HBM per device.

```python
import math
import jax
import jax.numpy as jnp
from jax import lax

SIDE = 128
NCLS = 96
ROT = 16
IMG_DEV = 256
NIMG = 8192
PIX = 16384
NREF = 1536


def template_views(key):
    base_key = jax.random.fold_in(key, 101)
    return jax.random.truncated_normal(base_key, -5.0, 5.0, (NREF, PIX), jnp.float32)


def draw_references(key, part):
    return template_views(key).astype(jnp.bfloat16)


def draw_images(key, part):
    views = template_views(key)
    pix_mean = jax.random.truncated_normal(jax.random.fold_in(key, 201), -3.0, 3.0, (PIX,), jnp.float32)
    pix_scale = jnp.exp(jax.random.uniform(jax.random.fold_in(key, 202), (PIX,), jnp.float32, 0.0, math.log(4.0)))
    chosen = 2 * jax.random.randint(jax.random.fold_in(key, 203), (NIMG,), 0, NREF // 2)
    signal = views[chosen]
    level = 0.005 + 0.02 * jnp.arange(NIMG, dtype=jnp.float32) / NIMG
    noise = jax.random.truncated_normal(jax.random.fold_in(key, 204), -5.0, 5.0, (NIMG, PIX), jnp.float32)
    img_scale = jnp.exp(jax.random.uniform(jax.random.fold_in(key, 205), (NIMG, 1), jnp.float32, math.log(0.5), math.log(2.0)))
    img_shift = 0.5 * jax.random.truncated_normal(jax.random.fold_in(key, 206), -4.0, 4.0, (NIMG, 1), jnp.float32)
    clean = level[:, None] * signal + noise
    return (img_shift + img_scale * (pix_mean[None, :] + pix_scale[None, :] * clean)).astype(jnp.bfloat16)


def draw_cycle_mask(key, part):
    index = jnp.arange(PIX, dtype=jnp.int32)
    row_pos = index // SIDE
    col_pos = index % SIDE
    distance = (2 * row_pos + 1 - SIDE) ** 2 + (2 * col_pos + 1 - SIDE) ** 2
    inner = jax.random.randint(jax.random.fold_in(key, 301), (), SIDE * 5 // 16, SIDE * 7 // 16 + 1)
    usable = jax.random.randint(jax.random.fold_in(key, 302), (PIX,), 0, 8)
    kept = (usable != 0) | (col_pos % 2 == 0)
    return ((distance >= (2 * inner) ** 2) & (distance < SIDE * SIDE) & kept).astype(jnp.int32)


def draw_view_class(key, part):
    order = jax.random.permutation(jax.random.fold_in(key, 401), NREF)
    return (order // ROT).astype(jnp.int32)


def setup_inputs(seed: int = 0) -> dict:
    arg_keys = jax.random.split(jax.random.key(seed), 5)
    images = draw_images(jax.random.fold_in(arg_keys[4], 71), 0)
    references = draw_references(jax.random.fold_in(arg_keys[4], 71), 0)
    cycle_mask = draw_cycle_mask(jax.random.fold_in(arg_keys[4], 71), 0)
    view_class = draw_view_class(jax.random.fold_in(arg_keys[4], 71), 0)
    return {"images": images, "references": references, "cycle_mask": cycle_mask, "view_class": view_class}


EPSILON = 1e-05

def reference(images, references, cycle_mask, view_class):
    total_images = images.shape[0]
    pixel_count = images.shape[1]
    blocks = images.reshape(total_images // IMG_DEV, IMG_DEV, pixel_count)

    def add_moments(carry, block):
        widened = block.astype(jnp.float32)
        return ((carry[0] + lax.optimization_barrier(jnp.sum(widened, 0)), carry[1] + lax.optimization_barrier(jnp.sum(widened * widened, 0))), None)
    zeros_pix = jnp.zeros((pixel_count,), jnp.float32)
    (col_sum, col_sq), _ = lax.scan(add_moments, (zeros_pix, zeros_pix), blocks)
    pix_mean = col_sum / total_images
    pix_std = jnp.sqrt(col_sq / total_images - pix_mean * pix_mean + EPSILON)
    cycle_weight = cycle_mask.astype(jnp.float32)
    cycle_count = jnp.sum(cycle_weight)
    ref_energy = lax.optimization_barrier(jnp.sum(jnp.square(references.astype(jnp.float32)), 1))
    onehot = (view_class[:, None] == jnp.arange(NCLS, dtype=jnp.int32)[None, :]).astype(jnp.float32)
    factor = 4.0 / SIDE

    def classify(carry, block):
        view_acc, class_acc = carry
        widened = block.astype(jnp.float32)
        whitened = (widened - pix_mean) / pix_std
        bg_mean = lax.optimization_barrier(jnp.sum(whitened * cycle_weight, 1)) / cycle_count
        bg_std = jnp.sqrt(lax.optimization_barrier(jnp.sum(whitened * whitened * cycle_weight, 1)) / cycle_count - bg_mean * bg_mean + EPSILON)
        normed = ((whitened - bg_mean[:, None]) / bg_std[:, None]).astype(jnp.bfloat16)
        raw = lax.dot_general(normed, references, (((1,), (1,)), ((), ())), preferred_element_type=jnp.float32)
        scores = (raw - 0.5 * ref_energy[None, :]) * factor
        row_max = lax.optimization_barrier(jnp.max(scores, 1, keepdims=True))
        log_total = row_max[:, 0] + jnp.log(lax.optimization_barrier(jnp.sum(jnp.exp(scores - row_max), 1)))
        evidence = log_total - lax.optimization_barrier(jnp.mean(scores, 1))
        posterior = jnp.exp(scores - log_total[:, None]).astype(jnp.bfloat16)
        view_acc = view_acc + lax.dot_general(posterior, normed, (((0,), (0,)), ((), ())), preferred_element_type=jnp.float32)
        class_mass = lax.optimization_barrier(jnp.sum(posterior, 0, dtype=jnp.float32))
        class_acc = class_acc + jnp.dot(class_mass, onehot, precision=lax.Precision.HIGHEST)
        return ((view_acc, class_acc), evidence)
    start_views = jnp.zeros((references.shape[0], pixel_count), jnp.float32)
    start_class = jnp.zeros((NCLS,), jnp.float32)
    (view_sums, class_total), evidence = lax.scan(classify, (start_views, start_class), blocks)
    return (view_sums, class_total * (NCLS / total_images), evidence.reshape(-1))
```

```python
import jax
import jax.numpy as jnp
from jax import lax
from jax.sharding import Mesh, PartitionSpec as P

SIDE = 128
NCLS = 96
EPSILON = 1e-05
BF16, F32 = jnp.bfloat16, jnp.float32
PAIR = [(0, 1), (1, 0)]


def fetch(value, axis, step):
    return lax.ppermute(value, axis, [((i + step) % 4, i) for i in range(4)])


def ring_order(slots, position):
    return [
        lax.select_n(position, *[slots[(place - p) % 4] for p in range(4)]) for place in range(4)
    ]


def spread_sum(value, axes, count):
    sent = jnp.broadcast_to(value[None], (count,) + value.shape)
    return jnp.sum(lax.all_to_all(sent, axes, split_axis=0, concat_axis=0), 0)


def on_device(images, references, cycle_mask, view_class):
    zl, x, y, core = (lax.axis_index(a) for a in ("zl", "x", "y", "c"))
    rows, wide = images.shape
    half = wide // 2
    views = references.shape[0]
    total_images = rows * 32
    mine = lambda a, axis: lax.dynamic_slice_in_dim(a, zl * half, half, axis)
    theirs = lambda a, axis: lax.dynamic_slice_in_dim(a, (1 - zl) * half, half, axis)
    swap = lambda a: lax.ppermute(a, "zl", PAIR)

    widened = images.astype(F32)
    local = jnp.stack([jnp.sum(widened, 0), jnp.sum(widened * widened, 0)])
    moments = mine(local, 1) + swap(theirs(local, 1))
    ref_other = swap(theirs(references, 1))
    ref_own = mine(references, 1)
    img_other = swap(theirs(images, 1))
    img_own = mine(images, 1)
    moments = spread_sum(moments, ("x", "y"), 16)

    a = jnp.where(zl == 0, ref_own, ref_other)
    b = jnp.where(zl == 0, ref_other, ref_own)
    a1 = jnp.stack(ring_order([a] + [fetch(a, "x", s) for s in (1, 2, 3)], x))
    b1 = jnp.stack(ring_order([b] + [fetch(b, "y", s) for s in (1, 2, 3)], y))
    a2 = jnp.stack(ring_order([a1] + [fetch(a1, "y", s) for s in (1, 2, 3)], y), 1)
    b2 = jnp.stack(ring_order([b1] + [fetch(b1, "x", s) for s in (1, 2, 3)], x), 0)
    refs = jnp.stack([a2, b2]).reshape(32 * views, half)

    shape = (4, 2, 32, half)
    own, other = img_own.reshape(shape), img_other.reshape(shape)
    pair = jnp.where(zl == 0, jnp.stack([own, other]), jnp.stack([other, own]))
    even, odd = pair[:, :, 0], pair[:, :, 1]
    block = jnp.where(core == 0, jnp.stack([even, odd]), jnp.stack([odd, even]))
    block = block.reshape(2 * rows, half)

    pix_mean = moments[0] / total_images
    pix_std = jnp.sqrt(moments[1] / total_images - pix_mean * pix_mean + EPSILON)
    whitened = (block.astype(F32) - pix_mean) / pix_std
    weight = mine(cycle_mask, 0).astype(F32)
    sums = jnp.stack([jnp.sum(whitened * weight, 1), jnp.sum(whitened * whitened * weight, 1)])
    sums = sums.reshape(2, 2, rows)
    sums = jnp.where(core == 0, sums, sums[:, ::-1])
    count = jnp.broadcast_to(jnp.sum(weight), (1, 2, rows))
    totals = spread_sum(jnp.concatenate([sums, count]).reshape(3, 2 * rows), ("zl", "zh", "c"), 16)
    totals = totals.reshape(3, 2, rows)
    totals = jnp.where(core == 0, totals, totals[:, ::-1]).reshape(3, 2 * rows)
    bg_mean = totals[0] / totals[2]
    bg_std = jnp.sqrt(totals[1] / totals[2] - bg_mean * bg_mean + EPSILON)
    normed = ((whitened - bg_mean[:, None]) / bg_std[:, None]).astype(BF16)

    ref_energy = jnp.sum(jnp.square(refs.astype(F32)), 1)
    raw = lax.dot_general(normed, refs, (((1,), (1,)), ((), ())), preferred_element_type=F32)
    partial_value = raw - 0.5 * ref_energy[None, :]
    both = partial_value[:rows] + lax.ppermute(partial_value[rows:], "c", PAIR)
    pieces = lax.all_to_all(both.reshape(8, 32, -1), ("zl", "zh"), split_axis=0, concat_axis=0)
    scores = jnp.sum(pieces, 0) * (4.0 / SIDE)

    row_max = jnp.max(scores, 1, keepdims=True)
    log_total = row_max[:, 0] + jnp.log(jnp.sum(jnp.exp(scores - row_max), 1))
    evidence = log_total - jnp.mean(scores, 1)
    posterior = jnp.exp(scores - log_total[:, None]).astype(BF16)

    gathered = lax.all_gather(posterior, ("zl", "zh"), axis=0, tiled=True)
    gathered = jnp.concatenate([gathered, lax.ppermute(gathered, "c", PAIR)])
    class_mass = jnp.sum(gathered, 0, dtype=F32)
    onehot = (view_class[:, None] == jnp.arange(NCLS, dtype=jnp.int32)[None, :]).astype(F32)
    share = jnp.dot(class_mass[None], onehot, precision=lax.Precision.HIGHEST)
    share = share + fetch(share, "x", 1) + fetch(share, "x", 2) + fetch(share, "x", 3)
    share = share + fetch(share, "y", 1) + fetch(share, "y", 2) + fetch(share, "y", 3)

    part = lax.dot_general(gathered, normed, (((0,), (0,)), ((), ())), preferred_element_type=F32)
    part = part.astype(BF16).reshape(2, 16, views, half)
    part = lax.all_to_all(
        part.reshape(32, views, half), ("zl", "x", "y"), split_axis=0, concat_axis=0
    )
    part = jnp.sum(part.reshape(2, 16, views, half).astype(F32), 1)
    view_sums = jnp.concatenate([part[0], part[1]], 1)
    return (view_sums, share[0] * (NCLS / total_images), evidence)


def solution(mesh):
    fine = Mesh(mesh.devices.reshape(2, 4, 4, 4, 2), ("zl", "x", "y", "zh", "c"))
    img, pix = ("zl", "x", "y"), ("zh", "c")
    in_specs = (P(img, pix), P(img, pix), P(pix), P())
    out_specs = (P(img, pix), P(), P(img + pix))
    return jax.shard_map(
        on_device, mesh=fine, in_specs=in_specs, out_specs=out_specs, check_vma=False
    )
```

```python
import jax
import jax.numpy as jnp
from jax import lax
from jax.sharding import Mesh, PartitionSpec as P

SIDE = 128
NCLS = 96
EPSILON = 1e-05
BF16, F32 = jnp.bfloat16, jnp.float32
PAIR = [(0, 1), (1, 0)]
FAR = [(zh, 4 + (zh - 1) % 4) for zh in range(4)] + [(4 + zh, (zh + 1) % 4) for zh in range(4)]


def place(zl, x, y):
    return zl * 16 + x * 4 + y


def plane(cross, step, first):
    pairs = []
    for zl in range(2):
        for x in range(4):
            for y in range(4):
                block = zl if first else zl ^ cross
                along_x = (block == 0) == first
                to = ((x - step) % 4, y) if along_x else (x, (y - step) % 4)
                pairs.append((place(zl, x, y), place(zl ^ cross if first else zl, *to)))
    return pairs


def ring_order(slots, position):
    return [
        lax.select_n(position, *[slots[(place - p) % 4] for p in range(4)]) for place in range(4)
    ]


def spread_sum(value, axes, count):
    sent = jnp.broadcast_to(value[None], (count,) + value.shape)
    return jnp.sum(lax.all_to_all(sent, axes, split_axis=0, concat_axis=0), 0)


def on_device(images, references, cycle_mask, view_class):
    zl, x, y, core = (lax.axis_index(a) for a in ("zl", "x", "y", "c"))
    rows, wide = images.shape
    half = wide // 2
    views = references.shape[0]
    total_images = rows * 32
    img = ("zl", "x", "y")
    mine = lambda a, axis: lax.dynamic_slice_in_dim(a, zl * half, half, axis)
    theirs = lambda a, axis: lax.dynamic_slice_in_dim(a, (1 - zl) * half, half, axis)
    swap = lambda a: lax.ppermute(a, "zl", PAIR)
    far = lambda a: lax.ppermute(a, ("zl", "zh"), FAR)

    widened = images.astype(F32)
    local = jnp.stack([jnp.sum(widened, 0), jnp.sum(widened * widened, 0)])
    moments = mine(local, 1) + swap(theirs(local, 1))
    ref_own, ref_other = mine(references, 1), theirs(references, 1)
    same = [ref_own] + [lax.ppermute(ref_own, img, plane(0, s, True)) for s in (1, 2, 3)]
    cross = [lax.ppermute(ref_other, img, plane(1, s, True)) for s in (0, 1, 2, 3)]
    img_other = swap(theirs(images, 1))
    img_own = mine(images, 1)
    moments = spread_sum(moments, ("x", "y"), 16)

    near = jnp.where(zl == 0, x, y)
    side = jnp.where(zl == 0, y, x)
    same = jnp.stack(ring_order(same, near))
    cross = jnp.stack(ring_order(cross, side))
    same2 = [same] + [lax.ppermute(same, img, plane(0, s, False)) for s in (1, 2, 3)]
    cross2 = [cross] + [lax.ppermute(cross, img, plane(1, s, False)) for s in (1, 2, 3)]
    shape = (4, 2, 32, half)
    own, other = img_own.reshape(shape), img_other.reshape(shape)
    pair = jnp.where(zl == 0, jnp.stack([own, other]), jnp.stack([other, own]))
    even, odd = pair[:, :, 0], pair[:, :, 1]
    block = jnp.where(core == 0, jnp.stack([even, odd]), jnp.stack([odd, even]))
    block = block.reshape(2 * rows, half)

    pix_mean = moments[0] / total_images
    pix_std = jnp.sqrt(moments[1] / total_images - pix_mean * pix_mean + EPSILON)
    whitened = (block.astype(F32) - pix_mean) / pix_std
    weight = mine(cycle_mask, 0).astype(F32)
    sums = jnp.stack([jnp.sum(whitened * weight, 1), jnp.sum(whitened * whitened * weight, 1)])
    sums = sums.reshape(2, 2, rows)
    sums = jnp.where(core == 0, sums, sums[:, ::-1])
    count = jnp.broadcast_to(jnp.sum(weight), (1, 2, rows))
    sums, same2, cross2 = lax.optimization_barrier((sums, same2, cross2))
    totals = spread_sum(jnp.concatenate([sums, count]).reshape(3, 2 * rows), ("zl", "zh", "c"), 16)
    totals = totals.reshape(3, 2, rows)
    totals = jnp.where(core == 0, totals, totals[:, ::-1]).reshape(3, 2 * rows)
    bg_mean = totals[0] / totals[2]
    bg_std = jnp.sqrt(totals[1] / totals[2] - bg_mean * bg_mean + EPSILON)
    normed = ((whitened - bg_mean[:, None]) / bg_std[:, None]).astype(BF16)

    same2, cross2 = ring_order(same2, side), ring_order(cross2, near)
    a = jnp.where(zl == 0, jnp.stack(same2, 1), jnp.stack(cross2, 1))
    b = jnp.where(zl == 0, jnp.stack(cross2), jnp.stack(same2))
    refs = jnp.stack([a, b]).reshape(32 * views, half)

    ref_energy = jnp.sum(jnp.square(refs.astype(F32)), 1)
    raw = lax.dot_general(normed, refs, (((1,), (1,)), ((), ())), preferred_element_type=F32)
    partial_value = raw - 0.5 * ref_energy[None, :]
    both = partial_value[:rows] + lax.ppermute(partial_value[rows:], "c", PAIR)
    both = both.reshape(2, rows // 2, 32 * views)
    cut = 16 * views
    kept = lax.dynamic_index_in_dim(both, zl, 0, False)
    sent = lax.dynamic_index_in_dim(both, 1 - zl, 0, False)
    kept = kept + jnp.concatenate([swap(sent[:, :cut]), far(sent[:, cut:])], 1)
    pieces = lax.all_to_all(kept.reshape(4, 32, -1), "zh", split_axis=0, concat_axis=0)
    scores = jnp.sum(pieces, 0) * (4.0 / SIDE)

    row_max = jnp.max(scores, 1, keepdims=True)
    log_total = row_max[:, 0] + jnp.log(jnp.sum(jnp.exp(scores - row_max), 1))
    evidence = log_total - jnp.mean(scores, 1)
    posterior = jnp.exp(scores - log_total[:, None]).astype(BF16)

    spread = jnp.broadcast_to(posterior[None], (4,) + posterior.shape)
    strip = lax.all_to_all(spread, "zh", split_axis=0, concat_axis=0).reshape(rows // 2, -1)
    other_strip = jnp.concatenate([swap(strip[:, :cut]), far(strip[:, cut:])], 1)
    gathered = jnp.where(
        zl == 0, jnp.concatenate([strip, other_strip]), jnp.concatenate([other_strip, strip])
    )
    gathered = jnp.concatenate([gathered, lax.ppermute(gathered, "c", PAIR)])

    part = lax.dot_general(gathered, normed, (((0,), (0,)), ((), ())), preferred_element_type=F32)
    part = part.astype(BF16).reshape(32, views, half)
    part, gathered = lax.optimization_barrier((part, gathered))
    part = lax.all_to_all(part, img, split_axis=0, concat_axis=0)
    class_mass = jnp.sum(gathered, 0, dtype=F32)
    onehot = (view_class[:, None] == jnp.arange(NCLS, dtype=jnp.int32)[None, :]).astype(F32)
    share = jnp.dot(class_mass[None], onehot, precision=lax.Precision.HIGHEST)
    share = spread_sum(share, ("x", "y"), 16)
    part = jnp.sum(part.reshape(2, 16, views, half).astype(F32), 1)
    view_sums = jnp.concatenate([part[0], part[1]], 1)
    return (view_sums, share[0] * (NCLS / total_images), evidence)


def solution(mesh):
    fine = Mesh(mesh.devices.reshape(2, 4, 4, 4, 2), ("zl", "x", "y", "zh", "c"))
    img, pix = ("zl", "x", "y"), ("zh", "c")
    in_specs = (P(img, pix), P(img, pix), P(pix), P())
    out_specs = (P(img, pix), P(), P(img + pix))
    return jax.shard_map(
        on_device, mesh=fine, in_specs=in_specs, out_specs=out_specs, check_vma=False
    )
```

```python
import jax
import jax.numpy as jnp
from jax import lax
from jax.sharding import Mesh, PartitionSpec as P

SIDE = 128
NCLS = 96
EPSILON = 1e-05
BF16, F32 = jnp.bfloat16, jnp.float32
PAIR = [(0, 1), (1, 0)]
FAR = [(zh, 4 + (zh - 1) % 4) for zh in range(4)] + [(4 + zh, (zh + 1) % 4) for zh in range(4)]


def place(zl, x, y):
    return zl * 16 + x * 4 + y


def plane(cross, step, first):
    pairs = []
    for zl in range(2):
        for x in range(4):
            for y in range(4):
                block = zl if first else zl ^ cross
                along_x = (block == 0) == first
                to = ((x - step) % 4, y) if along_x else (x, (y - step) % 4)
                pairs.append((place(zl, x, y), place(zl ^ cross if first else zl, *to)))
    return pairs


def ring_order(slots, position):
    return [
        lax.select_n(position, *[slots[(place - p) % 4] for p in range(4)]) for place in range(4)
    ]


def spread_sum(value, axes, count):
    sent = jnp.broadcast_to(value[None], (count,) + value.shape)
    return jnp.sum(lax.all_to_all(sent, axes, split_axis=0, concat_axis=0), 0)


def on_device(images, references, cycle_mask, view_class):
    zl, x, y, core = (lax.axis_index(a) for a in ("zl", "x", "y", "c"))
    rows, wide = images.shape
    half = wide // 2
    views = references.shape[0]
    total_images = rows * 32
    img = ("zl", "x", "y")
    mine = lambda a, axis: lax.dynamic_slice_in_dim(a, zl * half, half, axis)
    theirs = lambda a, axis: lax.dynamic_slice_in_dim(a, (1 - zl) * half, half, axis)
    swap = lambda a: lax.ppermute(a, "zl", PAIR)
    far = lambda a: lax.ppermute(a, ("zl", "zh"), FAR)

    widened = images.astype(F32)
    local = jnp.stack([jnp.sum(widened, 0), jnp.sum(widened * widened, 0)])
    moments = mine(local, 1) + swap(theirs(local, 1))
    ref_own, ref_other = mine(references, 1), theirs(references, 1)
    same = [ref_own] + [lax.ppermute(ref_own, img, plane(0, s, True)) for s in (1, 2, 3)]
    cross = [lax.ppermute(ref_other, img, plane(1, s, True)) for s in (0, 1, 2, 3)]
    img_other = swap(theirs(images, 1))
    img_own = mine(images, 1)
    moments = spread_sum(moments, ("x", "y"), 16)

    near = jnp.where(zl == 0, x, y)
    side = jnp.where(zl == 0, y, x)
    same = jnp.stack(ring_order(same, near))
    cross = jnp.stack(ring_order(cross, side))
    same2 = [same] + [lax.ppermute(same, img, plane(0, s, False)) for s in (1, 2, 3)]
    cross2 = [cross] + [lax.ppermute(cross, img, plane(1, s, False)) for s in (1, 2, 3)]

    shape = (4, 2, 32, half)
    own, other = img_own.reshape(shape), img_other.reshape(shape)
    pair = jnp.where(zl == 0, jnp.stack([own, other]), jnp.stack([other, own]))
    even, odd = pair[:, :, 0], pair[:, :, 1]
    block = jnp.where(core == 0, jnp.stack([even, odd]), jnp.stack([odd, even]))
    block = block.reshape(2 * rows, half)

    pix_mean = moments[0] / total_images
    pix_std = jnp.sqrt(moments[1] / total_images - pix_mean * pix_mean + EPSILON)
    whitened = (block.astype(F32) - pix_mean) / pix_std
    weight = mine(cycle_mask, 0).astype(F32)
    sums = jnp.stack([jnp.sum(whitened * weight, 1), jnp.sum(whitened * whitened * weight, 1)])
    sums = sums.reshape(2, 2, rows)
    sums = jnp.where(core == 0, sums, sums[:, ::-1])
    count = jnp.broadcast_to(jnp.sum(weight), (1, 2, rows))
    totals = spread_sum(jnp.concatenate([sums, count]).reshape(3, 2 * rows), ("zl", "zh", "c"), 16)
    totals = totals.reshape(3, 2, rows)
    totals = jnp.where(core == 0, totals, totals[:, ::-1]).reshape(3, 2 * rows)
    bg_mean = totals[0] / totals[2]
    bg_std = jnp.sqrt(totals[1] / totals[2] - bg_mean * bg_mean + EPSILON)
    normed = ((whitened - bg_mean[:, None]) / bg_std[:, None]).astype(BF16)

    same2, cross2 = ring_order(same2, side), ring_order(cross2, near)
    a = jnp.where(zl == 0, jnp.stack(same2, 1), jnp.stack(cross2, 1))
    b = jnp.where(zl == 0, jnp.stack(cross2), jnp.stack(same2))
    refs = jnp.stack([a, b]).reshape(32 * views, half)

    ref_energy = jnp.sum(jnp.square(refs.astype(F32)), 1)
    score = lambda a: (
        lax.dot_general(a, refs, (((1,), (1,)), ((), ())), preferred_element_type=F32)
        - 0.5 * ref_energy[None, :]
    )
    both = lax.ppermute(score(normed[rows:]), "c", PAIR)
    both = both + score(normed[:rows])
    both = both.reshape(2, rows // 2, 32 * views)
    cut = 16 * views
    kept = lax.dynamic_index_in_dim(both, zl, 0, False)
    sent = lax.dynamic_index_in_dim(both, 1 - zl, 0, False)
    kept = kept + jnp.concatenate([swap(sent[:, :cut]), far(sent[:, cut:])], 1)
    pieces = lax.all_to_all(kept.reshape(4, 32, -1), "zh", split_axis=0, concat_axis=0)
    scores = jnp.sum(pieces, 0) * (4.0 / SIDE)

    row_max = jnp.max(scores, 1, keepdims=True)
    log_total = row_max[:, 0] + jnp.log(jnp.sum(jnp.exp(scores - row_max), 1))
    evidence = log_total - jnp.mean(scores, 1)
    posterior = jnp.exp(scores - log_total[:, None]).astype(BF16)

    spread = jnp.broadcast_to(posterior[None], (4,) + posterior.shape)
    strip = lax.all_to_all(spread, "zh", split_axis=0, concat_axis=0).reshape(rows // 2, -1)
    class_mass = jnp.sum(strip, 0, dtype=F32)
    onehot = (view_class[:, None] == jnp.arange(NCLS, dtype=jnp.int32)[None, :]).astype(F32)
    share = jnp.dot(class_mass[None], onehot, precision=lax.Precision.HIGHEST)
    around = lambda a, axis: a + sum(
        lax.ppermute(a, axis, [(i, (i + s) % 4) for i in range(4)]) for s in (1, 2, 3)
    )
    share = around(share, "x")
    other_strip = [swap(strip[:, :cut]), far(strip[:, cut:])]
    other_strip = jnp.concatenate(other_strip, 1)
    gathered = jnp.where(
        zl == 0, jnp.concatenate([strip, other_strip]), jnp.concatenate([other_strip, strip])
    )
    gathered_c = lax.ppermute(gathered, "c", PAIR)
    gathered = jnp.concatenate([gathered, gathered_c])
    share = around(share, "y")
    share = share + swap(share)
    share = share + lax.ppermute(share, "c", PAIR)

    part = lax.dot_general(gathered, normed, (((0,), (0,)), ((), ())), preferred_element_type=F32)
    part = part.astype(BF16).reshape(32, views, half)
    part = lax.all_to_all(part, img, split_axis=0, concat_axis=0)
    part = jnp.sum(part.reshape(2, 16, views, half).astype(F32), 1)
    view_sums = jnp.concatenate([part[0], part[1]], 1)
    return (view_sums, share[0] * (NCLS / total_images), evidence)


def solution(mesh):
    fine = Mesh(mesh.devices.reshape(2, 4, 4, 4, 2), ("zl", "x", "y", "zh", "c"))
    img, pix = ("zl", "x", "y"), ("zh", "c")
    in_specs = (P(img, pix), P(img, pix), P(pix), P())
    out_specs = (P(img, pix), P(), P(img + pix))

    return jax.shard_map(
        on_device, mesh=fine, in_specs=in_specs, out_specs=out_specs, check_vma=False
    )
```

```python
import jax
import jax.numpy as jnp
from jax import lax
from jax.sharding import Mesh, PartitionSpec as P

SIDE = 128
NCLS = 96
EPSILON = 1e-05
BF16, F32 = jnp.bfloat16, jnp.float32
PAIR = [(0, 1), (1, 0)]
FAR = [(zh, 4 + (zh - 1) % 4) for zh in range(4)] + [(4 + zh, (zh + 1) % 4) for zh in range(4)]


def place(zl, x, y):
    return zl * 16 + x * 4 + y


def plane(cross, step, first):
    pairs = []
    for zl in range(2):
        for x in range(4):
            for y in range(4):
                block = zl if first else zl ^ cross
                along_x = (block == 0) == first
                to = ((x - step) % 4, y) if along_x else (x, (y - step) % 4)
                pairs.append((place(zl, x, y), place(zl ^ cross if first else zl, *to)))
    return pairs


def ring_order(slots, position):
    return [
        lax.select_n(position, *[slots[(place - p) % 4] for p in range(4)]) for place in range(4)
    ]


def spread(value, axes, count):
    sent = jnp.broadcast_to(value[None], (count,) + value.shape)
    return lax.all_to_all(sent, axes, split_axis=0, concat_axis=0)


def on_device(images, references, cycle_mask, view_class):
    zl, x, y, core = (lax.axis_index(a) for a in ("zl", "x", "y", "c"))
    rows, wide = images.shape
    half = wide // 2
    views = references.shape[0]
    total_images = rows * 32
    img = ("zl", "x", "y")
    mine = lambda a, axis: lax.dynamic_slice_in_dim(a, zl * half, half, axis)
    theirs = lambda a, axis: lax.dynamic_slice_in_dim(a, (1 - zl) * half, half, axis)
    swap = lambda a: lax.ppermute(a, "zl", PAIR)
    far = lambda a: lax.ppermute(a, ("zl", "zh"), FAR)

    widened = images.astype(F32)
    local = jnp.stack([jnp.sum(widened, 0), jnp.sum(widened * widened, 0)])
    moments = swap(theirs(local, 1))
    moments = mine(local, 1) + moments
    ref_own, ref_other = mine(references, 1), theirs(references, 1)
    same = [ref_own] + [lax.ppermute(ref_own, img, plane(0, s, True)) for s in (1, 2, 3)]
    cross = [lax.ppermute(ref_other, img, plane(1, s, True)) for s in (0, 1, 2, 3)]
    img_other = swap(theirs(images, 1))
    img_own = mine(images, 1)
    moments = jnp.sum(spread(moments, ("x", "y"), 16), 0)

    near = jnp.where(zl == 0, x, y)
    side = jnp.where(zl == 0, y, x)
    same = jnp.stack(ring_order(same, near))
    cross = jnp.stack(ring_order(cross, side))
    same2 = [same] + [lax.ppermute(same, img, plane(0, s, False)) for s in (1, 2, 3)]
    cross2 = [cross] + [lax.ppermute(cross, img, plane(1, s, False)) for s in (1, 2, 3)]

    shape = (4, 2, 32, half)
    own, other = img_own.reshape(shape), img_other.reshape(shape)
    pair = jnp.where(zl == 0, jnp.stack([own, other]), jnp.stack([other, own]))
    even, odd = pair[:, :, 0], pair[:, :, 1]
    block = jnp.where(core == 0, jnp.stack([even, odd]), jnp.stack([odd, even]))
    block = block.reshape(2 * rows, half)

    pix_mean = moments[0] / total_images
    pix_std = jnp.sqrt(moments[1] / total_images - pix_mean * pix_mean + EPSILON)
    whitened = (block.astype(F32) - pix_mean) / pix_std
    weight = mine(cycle_mask, 0).astype(F32)
    sums = jnp.stack([jnp.sum(whitened * weight, 1), jnp.sum(whitened * whitened * weight, 1)])
    sums = sums.reshape(2, 2, rows)
    sums = jnp.where(core == 0, sums, sums[:, ::-1])
    count = jnp.broadcast_to(jnp.sum(weight), (1, 2, rows))
    totals = spread(
        jnp.concatenate([sums, count]).reshape(3, 2 * rows), ("zl", "zh", "c"), 16
    )
    totals = jnp.sum(totals, 0)
    totals = totals.reshape(3, 2, rows)
    totals = jnp.where(core == 0, totals, totals[:, ::-1]).reshape(3, 2 * rows)
    bg_mean = totals[0] / totals[2]
    bg_std = jnp.sqrt(totals[1] / totals[2] - bg_mean * bg_mean + EPSILON)
    normed = ((whitened - bg_mean[:, None]) / bg_std[:, None]).astype(BF16)

    same2, cross2 = ring_order(same2, side), ring_order(cross2, near)
    a = jnp.where(zl == 0, jnp.stack(same2, 1), jnp.stack(cross2, 1))
    b = jnp.where(zl == 0, jnp.stack(cross2), jnp.stack(same2))
    refs = jnp.stack([a, b]).reshape(32 * views, half)

    ref_energy = jnp.sum(jnp.square(refs.astype(F32)), 1)
    score = lambda a: (
        lax.dot_general(a, refs, (((1,), (1,)), ((), ())), preferred_element_type=F32)
        - 0.5 * ref_energy[None, :]
    )
    both = lax.ppermute(score(normed[rows:]), "c", PAIR)
    both = both + lax.optimization_barrier(score(normed[:rows]))
    both = both.reshape(2, rows // 2, 32 * views)
    cut = 16 * views
    kept = lax.dynamic_index_in_dim(both, zl, 0, False)
    sent = lax.dynamic_index_in_dim(both, 1 - zl, 0, False)
    kept = kept + jnp.concatenate([swap(sent[:, :cut]), far(sent[:, cut:])], 1)
    pieces = lax.all_to_all(kept.reshape(4, 32, -1), "zh", split_axis=0, concat_axis=0)
    scores = jnp.sum(pieces, 0) * (4.0 / SIDE)

    row_max = jnp.max(scores, 1, keepdims=True)
    log_total = row_max[:, 0] + jnp.log(jnp.sum(jnp.exp(scores - row_max), 1))
    evidence = log_total - jnp.mean(scores, 1)
    posterior = jnp.exp(scores - log_total[:, None]).astype(BF16)

    strip = spread(posterior, "zh", 4).reshape(rows // 2, -1)
    class_mass = jnp.sum(strip, 0, dtype=F32)
    onehot = (view_class[:, None] == jnp.arange(NCLS, dtype=jnp.int32)[None, :]).astype(F32)
    share = jnp.dot(class_mass[None], onehot, precision=lax.Precision.HIGHEST)
    around = lambda a, axis: a + sum(
        lax.ppermute(a, axis, [(i, (i + s) % 4) for i in range(4)]) for s in (1, 2, 3)
    )
    share = around(share, "x")
    other_strip = [swap(strip[:, :cut]), far(strip[:, cut:])]
    other_strip = jnp.concatenate(other_strip, 1)
    gathered = jnp.where(
        zl == 0, jnp.concatenate([strip, other_strip]), jnp.concatenate([other_strip, strip])
    )
    gathered_c = lax.ppermute(gathered, "c", PAIR)
    gathered = jnp.concatenate([gathered, gathered_c])
    share = around(share, "y")
    share = share + swap(share)
    share = share + lax.ppermute(share, "c", PAIR)

    part = lax.dot_general(gathered, normed, (((0,), (0,)), ((), ())), preferred_element_type=F32)
    part = part.astype(BF16).reshape(32, views, half)
    part = lax.all_to_all(part, img, split_axis=0, concat_axis=0)
    part = jnp.sum(part.reshape(2, 16, views, half).astype(F32), 1)
    view_sums = jnp.concatenate([part[0], part[1]], 1)
    return (view_sums, share[0] * (NCLS / total_images), evidence)


def solution(mesh):
    fine = Mesh(mesh.devices.reshape(2, 4, 4, 4, 2), ("zl", "x", "y", "zh", "c"))
    img, pix = ("zl", "x", "y"), ("zh", "c")
    in_specs = (P(img, pix), P(img, pix), P(pix), P())
    out_specs = (P(img, pix), P(), P(img + pix))

    return jax.shard_map(
        on_device, mesh=fine, in_specs=in_specs, out_specs=out_specs, check_vma=False
    )
```

```python
import jax
import jax.numpy as jnp
from jax import lax
from jax.experimental import pallas as pl
from jax.experimental.pallas import tpu as pltpu
from jax.sharding import Mesh, PartitionSpec as P

SIDE = 128
NCLS = 96
EPSILON = 1e-05
BF16, F32 = jnp.bfloat16, jnp.float32
PAIR = [(0, 1), (1, 0)]
FAR = [(zh, 4 + (zh - 1) % 4) for zh in range(4)] + [(4 + zh, (zh + 1) % 4) for zh in range(4)]


def place(zl, x, y):
    return zl * 16 + x * 4 + y


def plane(cross, step, first):
    pairs = []
    for zl in range(2):
        for x in range(4):
            for y in range(4):
                block = zl if first else zl ^ cross
                along_x = (block == 0) == first
                to = ((x - step) % 4, y) if along_x else (x, (y - step) % 4)
                pairs.append((place(zl, x, y), place(zl ^ cross if first else zl, *to)))
    return pairs


def ring_order(slots, position):
    return [
        lax.select_n(position, *[slots[(place - p) % 4] for p in range(4)]) for place in range(4)
    ]


def place_kernel(at, *refs):
    for s in range(4):
        refs[4][(at[0] + s) % 4] = refs[s][...]


def by_place(at, *slots):
    vmem = pl.BlockSpec(memory_space=pltpu.VMEM)
    return pl.pallas_call(
        place_kernel,
        in_specs=[pl.BlockSpec(memory_space=pltpu.SMEM)] + [vmem] * 4,
        out_specs=vmem,
        out_shape=jax.ShapeDtypeStruct((4,) + slots[0].shape, slots[0].dtype),
    )(at.reshape(1), *slots)


def spread(value, axes, count):
    sent = jnp.broadcast_to(value[None], (count,) + value.shape)
    return lax.all_to_all(sent, axes, split_axis=0, concat_axis=0)


def on_device(images, references, cycle_mask, view_class):
    zl, x, y, zh, core = (lax.axis_index(a) for a in ("zl", "x", "y", "zh", "c"))
    rows, wide = images.shape
    half = wide // 2
    views = references.shape[0]
    total_images = rows * 32
    img = ("zl", "x", "y")
    mine = lambda a, axis: lax.dynamic_slice_in_dim(a, zl * half, half, axis)
    theirs = lambda a, axis: lax.dynamic_slice_in_dim(a, (1 - zl) * half, half, axis)
    swap = lambda a: lax.ppermute(a, "zl", PAIR)
    far = lambda a: lax.ppermute(a, ("zl", "zh"), FAR)

    widened = images.astype(F32)
    local = jnp.stack([jnp.sum(widened, 0), jnp.sum(widened * widened, 0)])
    moments = swap(theirs(local, 1))
    moments = mine(local, 1) + moments
    ref_own, ref_other = mine(references, 1), theirs(references, 1)
    same = [ref_own] + [lax.ppermute(ref_own, img, plane(0, s, True)) for s in (1, 2, 3)]
    cross = [lax.ppermute(ref_other, img, plane(1, s, True)) for s in (0, 1, 2, 3)]
    img_other = swap(theirs(images, 1))
    img_own = mine(images, 1)
    moments = jnp.sum(spread(moments, ("x", "y"), 16), 0)

    near = jnp.where(zl == 0, x, y)
    side = jnp.where(zl == 0, y, x)
    same = jnp.stack(ring_order(same, near))
    cross = jnp.stack(ring_order(cross, side))
    same2 = [same] + [lax.ppermute(same, img, plane(0, s, False)) for s in (1, 2, 3)]
    cross2 = [cross] + [lax.ppermute(cross, img, plane(1, s, False)) for s in (1, 2, 3)]

    shape = (4, 2, 2, 16, half)
    own, other = img_own.reshape(shape), img_other.reshape(shape)
    pair = jnp.where(zl == 0, jnp.stack([own, other]), jnp.stack([other, own]))
    first = jnp.where(core == 0, pair[:, :, 0], pair[:, :, 1])
    second = jnp.where(core == 0, pair[:, :, 1], pair[:, :, 0])
    block = jnp.stack([r[:, :, h] for h in range(2) for r in (first, second)])
    block = block.reshape(2 * rows, half)

    pix_mean = moments[0] / total_images
    pix_std = jnp.sqrt(moments[1] / total_images - pix_mean * pix_mean + EPSILON)
    whitened = (block.astype(F32) - pix_mean) / pix_std
    weight = mine(cycle_mask, 0).astype(F32)
    sums = jnp.stack([jnp.sum(whitened * weight, 1), jnp.sum(whitened * whitened * weight, 1)])
    sums = sums.reshape(2, 2, 2, rows // 2)
    sums = jnp.where(core == 0, sums, sums[:, :, ::-1])
    count = jnp.broadcast_to(jnp.sum(weight), (1, 2, 2, rows // 2))
    totals = spread(
        jnp.concatenate([sums, count]).reshape(3, 2 * rows), ("zl", "zh", "c"), 16
    )
    totals = jnp.sum(totals, 0)
    totals = totals.reshape(3, 2, 2, rows // 2)
    totals = jnp.where(core == 0, totals, totals[:, :, ::-1]).reshape(3, 2 * rows)
    bg_mean = totals[0] / totals[2]
    bg_std = jnp.sqrt(totals[1] / totals[2] - bg_mean * bg_mean + EPSILON)
    normed = ((whitened - bg_mean[:, None]) / bg_std[:, None]).astype(BF16)

    same2, cross2 = ring_order(same2, side), ring_order(cross2, near)
    a = jnp.where(zl == 0, jnp.stack(same2, 1), jnp.stack(cross2, 1))
    b = jnp.where(zl == 0, jnp.stack(cross2), jnp.stack(same2))
    refs = jnp.stack([a, b]).reshape(32 * views, half)

    ref_energy = jnp.sum(jnp.square(refs.astype(F32)), 1)
    score = lambda a: (
        lax.dot_general(a, refs, (((1,), (1,)), ((), ())), preferred_element_type=F32)
        - 0.5 * ref_energy[None, :]
    )
    quarter, every = rows // 4, 32 * views
    cut = quarter // 2
    forward = lambda a, s: lax.ppermute(a, "zh", [(i, (i + s) % 4) for i in range(4)])
    backward = lambda a, s: lax.ppermute(a, "zh", [((i + s) % 4, i) for i in range(4)])
    normed_parts = normed.reshape(2, 2, 2 * quarter, half)
    kept, posteriors, strips, gathered = [], [], [], []
    evidence = []
    behind = lambda a, done: lax.optimization_barrier((a, done[0]))[0] if done else a
    sums = []
    for h in range(2):
        both = lax.ppermute(score(normed_parts[h, 1]), "c", PAIR)
        sums.append(both + lax.optimization_barrier(score(normed_parts[h, 0])))
    for h in range(2):
        both = sums[h]
        rows_at = lambda start, count: lax.dynamic_slice_in_dim(both, start, count)
        leave = (1 - zl) * quarter
        came = [swap(rows_at(leave, cut)), far(rows_at(leave + cut, cut))]
        came = behind(came, kept)
        kept.append(rows_at(zl * quarter, quarter) + jnp.concatenate(came))
    for h in range(2):
        take = lambda s: lax.dynamic_slice_in_dim(kept[h], (zh + s) % 4 * 16, 16)
        came = [forward(take(s), s) for s in (1, 2, 3)]
        came = behind(came, posteriors)
        score_rows = (take(0) + came[0] + came[1] + came[2]) * (4.0 / SIDE)
        row_max = jnp.max(score_rows, 1, keepdims=True)
        log_total = row_max[:, 0] + jnp.log(jnp.sum(jnp.exp(score_rows - row_max), 1))
        evidence.append(log_total - jnp.mean(score_rows, 1))
        posteriors.append(jnp.exp(score_rows - log_total[:, None]).astype(BF16))
    for h in range(2):
        slots = [backward(posteriors[h], s) for s in (1, 2, 3)]
        slots = behind(slots, strips)
        strips.append(by_place(zh, posteriors[h], *slots))
    class_mass = sum(jnp.sum(a, (0, 1), dtype=F32) for a in strips)
    onehot = (view_class[:, None] == jnp.arange(NCLS, dtype=jnp.int32)[None, :]).astype(F32)
    share = jnp.dot(class_mass[None], onehot, precision=lax.Precision.HIGHEST)
    around = lambda a, axis: a + sum(
        lax.ppermute(a, axis, [(i, (i + s) % 4) for i in range(4)]) for s in (1, 2, 3)
    )
    share = around(share, "x")
    for h in range(2):
        strip = strips[h].reshape(2, cut, every)
        came = [swap(strip[0]), far(strip[1])]
        came = jnp.stack(behind(came, gathered))
        both = jnp.where(zl == 0, jnp.stack([strip, came]), jnp.stack([came, strip]))
        both = both.reshape(2 * quarter, every)
        gathered += [both, lax.ppermute(both, "c", PAIR)]
    gathered = jnp.concatenate(gathered)
    share = around(share, "y")
    share = share + swap(share)
    share = share + lax.ppermute(share, "c", PAIR)

    part = lax.dot_general(gathered, normed, (((0,), (0,)), ((), ())), preferred_element_type=F32)
    part = part.astype(BF16).reshape(32, views, half)
    part = lax.all_to_all(part, img, split_axis=0, concat_axis=0)
    part = jnp.sum(part.reshape(2, 16, views, half).astype(F32), 1)
    view_sums = jnp.concatenate([part[0], part[1]], 1)
    return (view_sums, share[0] * (NCLS / total_images), jnp.concatenate(evidence))


def solution(mesh):
    fine = Mesh(mesh.devices.reshape(2, 4, 4, 4, 2), ("zl", "x", "y", "zh", "c"))
    img, pix = ("zl", "x", "y"), ("zh", "c")
    in_specs = (P(img, pix), P(img, pix), P(pix), P())
    out_specs = (P(img, pix), P(), P(img + pix))

    return jax.shard_map(
        on_device, mesh=fine, in_specs=in_specs, out_specs=out_specs, check_vma=False
    )
```

```python
import jax
import jax.numpy as jnp
from jax import lax
from jax.experimental import pallas as pl
from jax.experimental.pallas import tpu as pltpu
from jax.sharding import Mesh, PartitionSpec as P

SIDE = 128
NCLS = 96
EPSILON = 1e-05
BF16, F32 = jnp.bfloat16, jnp.float32
PAIR = [(0, 1), (1, 0)]
FAR = [(zh, 4 + (zh - 1) % 4) for zh in range(4)] + [(4 + zh, (zh + 1) % 4) for zh in range(4)]


def place(zl, x, y):
    return zl * 16 + x * 4 + y


def plane(cross, step, first):
    pairs = []
    for zl in range(2):
        for x in range(4):
            for y in range(4):
                block = zl if first else zl ^ cross
                along_x = (block == 0) == first
                to = ((x - step) % 4, y) if along_x else (x, (y - step) % 4)
                pairs.append((place(zl, x, y), place(zl ^ cross if first else zl, *to)))
    return pairs


def ring_order(slots, position):
    return [
        lax.select_n(position, *[slots[(place - p) % 4] for p in range(4)]) for place in range(4)
    ]


def put_kernel(at, *refs):
    out = refs[8]
    for group in range(2):
        block = (at[0] + group) % 2
        for s in range(4):
            p = (at[1 + group] + s) % 4
            for j in range(4):
                out[jnp.where(block == 0, j * 4 + p, 16 + p * 4 + j)] = refs[4 * group + s][j]


def put_together(at, parts):
    vmem = pl.BlockSpec(memory_space=pltpu.VMEM)
    return pl.pallas_call(
        put_kernel,
        in_specs=[pl.BlockSpec(memory_space=pltpu.SMEM)] + [vmem] * 8,
        out_specs=vmem,
        out_shape=jax.ShapeDtypeStruct((32,) + parts[0].shape[1:], parts[0].dtype),
    )(at, *parts)


def spread(value, axes, count):
    sent = jnp.broadcast_to(value[None], (count,) + value.shape)
    return lax.all_to_all(sent, axes, split_axis=0, concat_axis=0)


def on_device(images, references, cycle_mask, view_class):
    zl, x, y, core = (lax.axis_index(a) for a in ("zl", "x", "y", "c"))
    rows, wide = images.shape
    half = wide // 2
    views = references.shape[0]
    total_images = rows * 32
    img = ("zl", "x", "y")
    mine = lambda a, axis: lax.dynamic_slice_in_dim(a, zl * half, half, axis)
    theirs = lambda a, axis: lax.dynamic_slice_in_dim(a, (1 - zl) * half, half, axis)
    swap = lambda a: lax.ppermute(a, "zl", PAIR)
    far = lambda a: lax.ppermute(a, ("zl", "zh"), FAR)

    widened = images.astype(F32)
    local = jnp.stack([jnp.sum(widened, 0), jnp.sum(widened * widened, 0)])
    moments = swap(theirs(local, 1))
    moments = mine(local, 1) + moments
    ref_own, ref_other = mine(references, 1), theirs(references, 1)
    same = [ref_own] + [lax.ppermute(ref_own, img, plane(0, s, True)) for s in (1, 2, 3)]
    cross = [lax.ppermute(ref_other, img, plane(1, s, True)) for s in (0, 1, 2, 3)]
    img_other = swap(theirs(images, 1))
    img_own = mine(images, 1)
    moments = jnp.sum(spread(moments, ("x", "y"), 16), 0)

    near = jnp.where(zl == 0, x, y)
    side = jnp.where(zl == 0, y, x)
    same = jnp.stack(ring_order(same, near))
    cross = jnp.stack(ring_order(cross, side))
    same2 = [same] + [lax.ppermute(same, img, plane(0, s, False)) for s in (1, 2, 3)]
    cross2 = [cross] + [lax.ppermute(cross, img, plane(1, s, False)) for s in (1, 2, 3)]

    shape = (4, 2, 32, half)
    own, other = img_own.reshape(shape), img_other.reshape(shape)
    pair = jnp.where(zl == 0, jnp.stack([own, other]), jnp.stack([other, own]))
    even, odd = pair[:, :, 0], pair[:, :, 1]
    block = jnp.where(core == 0, jnp.stack([even, odd]), jnp.stack([odd, even]))
    block = block.reshape(2 * rows, half)

    pix_mean = moments[0] / total_images
    pix_std = jnp.sqrt(moments[1] / total_images - pix_mean * pix_mean + EPSILON)
    whitened = (block.astype(F32) - pix_mean) / pix_std
    weight = mine(cycle_mask, 0).astype(F32)
    sums = jnp.stack([jnp.sum(whitened * weight, 1), jnp.sum(whitened * whitened * weight, 1)])
    sums = sums.reshape(2, 2, rows)
    sums = jnp.where(core == 0, sums, sums[:, ::-1])
    count = jnp.broadcast_to(jnp.sum(weight), (1, 2, rows))
    sums = jnp.concatenate([sums, count]).reshape(3, 2 * rows)
    sums = sums + lax.ppermute(sums, "c", PAIR)
    totals = spread(sums, ("zl", "zh"), 8)
    totals = jnp.sum(totals, 0)
    totals = totals.reshape(3, 2, rows)
    totals = jnp.where(core == 0, totals, totals[:, ::-1]).reshape(3, 2 * rows)
    bg_mean = totals[0] / totals[2]
    bg_std = jnp.sqrt(totals[1] / totals[2] - bg_mean * bg_mean + EPSILON)
    normed = ((whitened - bg_mean[:, None]) / bg_std[:, None]).astype(BF16)

    refs = put_together(jnp.stack([zl, side, near]), same2 + cross2)
    refs = refs.reshape(32 * views, half)
    ref_energy = jnp.sum(jnp.square(refs.astype(F32)), 1)
    score = lambda a: (
        lax.dot_general(a, refs, (((1,), (1,)), ((), ())), preferred_element_type=F32)
        - 0.5 * ref_energy[None, :]
    )
    both = lax.ppermute(score(normed[rows:]), "c", PAIR)
    both = both + lax.optimization_barrier(score(normed[:rows]))
    both = both.reshape(2, rows // 2, 32 * views)
    cut = 16 * views
    kept = lax.dynamic_index_in_dim(both, zl, 0, False)
    sent = lax.dynamic_index_in_dim(both, 1 - zl, 0, False)
    kept = kept + jnp.concatenate([swap(sent[:, :cut]), far(sent[:, cut:])], 1)
    pieces = lax.all_to_all(kept.reshape(4, 32, -1), "zh", split_axis=0, concat_axis=0)
    scores = jnp.sum(pieces, 0) * (4.0 / SIDE)

    row_max = jnp.max(scores, 1, keepdims=True)
    log_total = row_max[:, 0] + jnp.log(jnp.sum(jnp.exp(scores - row_max), 1))
    evidence = log_total - jnp.mean(scores, 1)
    posterior = jnp.exp(scores - log_total[:, None]).astype(BF16)

    strip = spread(posterior, "zh", 4).reshape(rows // 2, -1)
    class_mass = jnp.sum(strip, 0, dtype=F32)
    onehot = (view_class[:, None] == jnp.arange(NCLS, dtype=jnp.int32)[None, :]).astype(F32)
    share = jnp.dot(class_mass[None], onehot, precision=lax.Precision.HIGHEST)
    share = spread(share, ("x", "y"), 16)
    share = jnp.sum(share, 0)
    other_strip = [swap(strip[:, :cut]), far(strip[:, cut:])]
    other_strip = jnp.concatenate(other_strip, 1)
    gathered = jnp.where(
        zl == 0, jnp.concatenate([strip, other_strip]), jnp.concatenate([other_strip, strip])
    )
    gathered_c = lax.ppermute(gathered, "c", PAIR)
    gathered = jnp.concatenate([gathered, gathered_c])
    share = share + swap(share)
    share = share + lax.ppermute(share, "c", PAIR)

    part = lax.dot_general(gathered, normed, (((0,), (0,)), ((), ())), preferred_element_type=F32)
    part = part.astype(BF16).reshape(32, views, half)
    part = lax.all_to_all(part, img, split_axis=0, concat_axis=0)
    part = jnp.sum(part.reshape(2, 16, views, half).astype(F32), 1)
    view_sums = jnp.concatenate([part[0], part[1]], 1)
    return (view_sums, share[0] * (NCLS / total_images), evidence)


def solution(mesh):
    fine = Mesh(mesh.devices.reshape(2, 4, 4, 4, 2), ("zl", "x", "y", "zh", "c"))
    img, pix = ("zl", "x", "y"), ("zh", "c")
    in_specs = (P(img, pix), P(img, pix), P(pix), P())
    out_specs = (P(img, pix), P(), P(img + pix))

    return jax.shard_map(
        on_device, mesh=fine, in_specs=in_specs, out_specs=out_specs, check_vma=False
    )
```

```python
import jax
import jax.numpy as jnp
from jax import lax
from jax.experimental import pallas as pl
from jax.experimental.pallas import tpu as pltpu
from jax.sharding import Mesh, PartitionSpec as P

SIDE = 128
NCLS = 96
EPSILON = 1e-05
BF16, F32 = jnp.bfloat16, jnp.float32
PAIR = [(0, 1), (1, 0)]
FAR = [(zh, 4 + (zh - 1) % 4) for zh in range(4)] + [(4 + zh, (zh + 1) % 4) for zh in range(4)]


def plane(step, first):
    pairs = []
    for x in range(4):
        for y in range(4):
            for core in range(2):
                along_x = (core == 0) == first
                to = ((x - step) % 4, y) if along_x else (x, (y - step) % 4)
                pairs.append((x * 8 + y * 2 + core, to[0] * 8 + to[1] * 2 + core))
    return pairs


def put_kernel(at, *refs):
    out = refs[4]
    zl, core, first, second = at[0], at[1], at[2], at[3]
    rows = out.shape[1]
    for t in range(4):
        q = (second + t) % 4
        for s in range(4):
            p = (first + s) % 4
            spot = jnp.where(core == 0, p * 4 + q, q * 4 + p)
            for k in range(2):
                out[(zl + k) % 2 * 16 + spot] = refs[t][s, k * rows : (k + 1) * rows]


def put_together(at, parts):
    vmem = pl.BlockSpec(memory_space=pltpu.VMEM)
    shape = (32, parts[0].shape[1] // 2, parts[0].shape[2])
    return pl.pallas_call(
        put_kernel,
        in_specs=[pl.BlockSpec(memory_space=pltpu.SMEM)] + [vmem] * 4,
        out_specs=vmem,
        out_shape=jax.ShapeDtypeStruct(shape, parts[0].dtype),
    )(at, *parts)


def spread(value, axes, count):
    sent = jnp.broadcast_to(value[None], (count,) + value.shape)
    return lax.all_to_all(sent, axes, split_axis=0, concat_axis=0)


def on_device(images, references, cycle_mask, view_class):
    zl, x, y, core = (lax.axis_index(a) for a in ("zl", "x", "y", "c"))
    rows, wide = images.shape
    half = wide // 2
    views = references.shape[0]
    total_images = rows * 32
    img = ("zl", "x", "y")
    mine = lambda a, axis: lax.dynamic_slice_in_dim(a, zl * half, half, axis)
    theirs = lambda a, axis: lax.dynamic_slice_in_dim(a, (1 - zl) * half, half, axis)
    swap = lambda a: lax.ppermute(a, "zl", PAIR)
    far = lambda a: lax.ppermute(a, ("zl", "zh"), FAR)

    widened = images.astype(F32)
    local = jnp.stack([jnp.sum(widened, 0), jnp.sum(widened * widened, 0)])
    moments = swap(theirs(local, 1))
    moments = mine(local, 1) + moments
    plan = ("x", "y", "c")
    ref_other = swap(theirs(references, 1))
    ref_pair = jnp.concatenate([mine(references, 1), ref_other])
    line = [lax.ppermute(ref_pair, plan, plane(s, True)) for s in (1, 2, 3)]
    img_other = swap(theirs(images, 1))
    img_own = mine(images, 1)
    moments = spread(moments, ("x", "y"), 16)
    moments = jnp.sum(moments, 0)

    line = jnp.stack([ref_pair] + line)
    sheet = [line] + [lax.ppermute(line, plan, plane(s, False)) for s in (1, 2, 3)]

    shape = (4, 2, 32, half)
    own, other = img_own.reshape(shape), img_other.reshape(shape)
    pair = jnp.where(zl == 0, jnp.stack([own, other]), jnp.stack([other, own]))
    even, odd = pair[:, :, 0], pair[:, :, 1]
    block = jnp.where(core == 0, jnp.stack([even, odd]), jnp.stack([odd, even]))
    block = block.reshape(2 * rows, half)

    pix_mean = moments[0] / total_images
    pix_std = jnp.sqrt(moments[1] / total_images - pix_mean * pix_mean + EPSILON)
    whitened = (block.astype(F32) - pix_mean) / pix_std
    weight = mine(cycle_mask, 0).astype(F32)
    sums = jnp.stack([jnp.sum(whitened * weight, 1), jnp.sum(whitened * whitened * weight, 1)])
    sums = sums.reshape(2, 2, rows)
    sums = jnp.where(core == 0, sums, sums[:, ::-1])
    count = jnp.broadcast_to(jnp.sum(weight), (1, 2, rows))
    sums = jnp.concatenate([sums, count]).reshape(3, 2 * rows)
    sums = sums + lax.ppermute(sums, "c", PAIR)
    totals = spread(sums, ("zl", "zh"), 8)
    totals = jnp.sum(totals, 0)
    totals = totals.reshape(3, 2, rows)
    totals = jnp.where(core == 0, totals, totals[:, ::-1]).reshape(3, 2 * rows)
    bg_mean = totals[0] / totals[2]
    bg_std = jnp.sqrt(totals[1] / totals[2] - bg_mean * bg_mean + EPSILON)
    normed = ((whitened - bg_mean[:, None]) / bg_std[:, None]).astype(BF16)

    first, second = jnp.where(core == 0, x, y), jnp.where(core == 0, y, x)
    refs = put_together(jnp.stack([zl, core, first, second]), sheet)
    refs = refs.reshape(32 * views, half)
    ref_energy = jnp.sum(jnp.square(refs.astype(F32)), 1)
    score = lambda a: (
        lax.dot_general(a, refs, (((1,), (1,)), ((), ())), preferred_element_type=F32)
        - 0.5 * ref_energy[None, :]
    )
    both = lax.ppermute(score(normed[rows:]), "c", PAIR)
    both = both + lax.optimization_barrier(score(normed[:rows]))
    both = both.reshape(2, rows // 2, 32 * views)
    cut = 16 * views
    kept = lax.dynamic_index_in_dim(both, zl, 0, False)
    sent = lax.dynamic_index_in_dim(both, 1 - zl, 0, False)
    kept = kept + jnp.concatenate([swap(sent[:, :cut]), far(sent[:, cut:])], 1)
    pieces = lax.all_to_all(kept.reshape(4, 32, -1), "zh", split_axis=0, concat_axis=0)
    scores = jnp.sum(pieces, 0) * (4.0 / SIDE)

    row_max = jnp.max(scores, 1, keepdims=True)
    log_total = row_max[:, 0] + jnp.log(jnp.sum(jnp.exp(scores - row_max), 1))
    evidence = log_total - jnp.mean(scores, 1)
    posterior = jnp.exp(scores - log_total[:, None]).astype(BF16)

    strip = spread(posterior, "zh", 4).reshape(rows // 2, -1)
    class_mass = jnp.sum(strip, 0, dtype=F32)
    onehot = (view_class[:, None] == jnp.arange(NCLS, dtype=jnp.int32)[None, :]).astype(F32)
    share = jnp.dot(class_mass[None], onehot, precision=lax.Precision.HIGHEST)
    share = spread(share, ("x", "y"), 16)
    share = jnp.sum(share, 0)
    other_strip = [swap(strip[:, :cut]), far(strip[:, cut:])]
    other_strip = jnp.concatenate(other_strip, 1)
    gathered = jnp.where(
        zl == 0, jnp.concatenate([strip, other_strip]), jnp.concatenate([other_strip, strip])
    )
    gathered_c = lax.ppermute(gathered, "c", PAIR)
    gathered = jnp.concatenate([gathered, gathered_c])
    share = share + swap(share)
    share = share + lax.ppermute(share, "c", PAIR)

    part = lax.dot_general(gathered, normed, (((0,), (0,)), ((), ())), preferred_element_type=F32)
    part = part.astype(BF16).reshape(32, views, half)
    part = lax.all_to_all(part, img, split_axis=0, concat_axis=0)
    part = jnp.sum(part.reshape(2, 16, views, half).astype(F32), 1)
    view_sums = jnp.concatenate([part[0], part[1]], 1)
    return (view_sums, share[0] * (NCLS / total_images), evidence)


def solution(mesh):
    fine = Mesh(mesh.devices.reshape(2, 4, 4, 4, 2), ("zl", "x", "y", "zh", "c"))
    img, pix = ("zl", "x", "y"), ("zh", "c")
    in_specs = (P(img, pix), P(img, pix), P(pix), P())
    out_specs = (P(img, pix), P(), P(img + pix))

    return jax.shard_map(
        on_device, mesh=fine, in_specs=in_specs, out_specs=out_specs, check_vma=False
    )
```

```python
import jax
import jax.numpy as jnp
from jax import lax
from jax.experimental import pallas as pl
from jax.experimental.pallas import tpu as pltpu
from jax.sharding import Mesh, PartitionSpec as P

SIDE = 128
NCLS = 96
EPSILON = 1e-05
BF16, F32 = jnp.bfloat16, jnp.float32
PAIR = [(0, 1), (1, 0)]
FAR = [(zh, 4 + (zh - 1) % 4) for zh in range(4)] + [(4 + zh, (zh + 1) % 4) for zh in range(4)]


def plane(step, first):
    pairs = []
    for x in range(4):
        for y in range(4):
            for core in range(2):
                along_x = (core == 0) == first
                to = ((x - step) % 4, y) if along_x else (x, (y - step) % 4)
                pairs.append((x * 8 + y * 2 + core, to[0] * 8 + to[1] * 2 + core))
    return pairs


def put_kernel(at, *refs):
    out = refs[4]
    zl, core, first, second = at[0], at[1], at[2], at[3]
    rows = out.shape[1]
    for t in range(4):
        q = (second + t) % 4
        for s in range(4):
            p = (first + s) % 4
            spot = jnp.where(core == 0, p * 4 + q, q * 4 + p)
            for k in range(2):
                out[(zl + k) % 2 * 16 + spot] = refs[t][s, k * rows : (k + 1) * rows]


def put_together(at, parts):
    vmem = pl.BlockSpec(memory_space=pltpu.VMEM)
    shape = (32, parts[0].shape[1] // 2, parts[0].shape[2])
    return pl.pallas_call(
        put_kernel,
        in_specs=[pl.BlockSpec(memory_space=pltpu.SMEM)] + [vmem] * 4,
        out_specs=vmem,
        out_shape=jax.ShapeDtypeStruct(shape, parts[0].dtype),
    )(at, *parts)


def spread(value, axes, count):
    sent = jnp.broadcast_to(value[None], (count,) + value.shape)
    return lax.all_to_all(sent, axes, split_axis=0, concat_axis=0)


def on_device(images, references, cycle_mask, view_class):
    zl, x, y, zh, core = (lax.axis_index(a) for a in ("zl", "x", "y", "zh", "c"))
    rows, wide = images.shape
    half = wide // 2
    views = references.shape[0]
    total_images = rows * 32
    img = ("zl", "x", "y")
    mine = lambda a, axis: lax.dynamic_slice_in_dim(a, zl * half, half, axis)
    theirs = lambda a, axis: lax.dynamic_slice_in_dim(a, (1 - zl) * half, half, axis)
    swap = lambda a: lax.ppermute(a, "zl", PAIR)
    far = lambda a: lax.ppermute(a, ("zl", "zh"), FAR)

    widened = images.astype(F32)
    local = jnp.stack([jnp.sum(widened, 0), jnp.sum(widened * widened, 0)])
    moments = swap(theirs(local, 1))
    moments = mine(local, 1) + moments
    plan = ("x", "y", "c")
    ref_other = swap(theirs(references, 1))
    ref_pair = jnp.concatenate([mine(references, 1), ref_other])
    line = [lax.ppermute(ref_pair, plan, plane(s, True)) for s in (1, 2, 3)]
    img_other = swap(theirs(images, 1))
    img_own = mine(images, 1)
    moments = spread(moments, ("x", "y"), 16)
    moments = jnp.sum(moments, 0)

    line = jnp.stack([ref_pair] + line)
    sheet = [line] + [lax.ppermute(line, plan, plane(s, False)) for s in (1, 2, 3)]

    shape = (4, 2, 32, half)
    own, other = img_own.reshape(shape), img_other.reshape(shape)
    pair = jnp.where(zl == 0, jnp.stack([own, other]), jnp.stack([other, own]))
    even, odd = pair[:, :, 0], pair[:, :, 1]
    block = jnp.where(core == 0, jnp.stack([even, odd]), jnp.stack([odd, even]))
    block = block.reshape(2 * rows, half)

    pix_mean = moments[0] / total_images
    pix_std = jnp.sqrt(moments[1] / total_images - pix_mean * pix_mean + EPSILON)
    whitened = (block.astype(F32) - pix_mean) / pix_std
    weight = mine(cycle_mask, 0).astype(F32)
    sums = jnp.stack([jnp.sum(whitened * weight, 1), jnp.sum(whitened * whitened * weight, 1)])
    sums = sums.reshape(2, 2, rows)
    sums = jnp.where(core == 0, sums, sums[:, ::-1])
    count = jnp.broadcast_to(jnp.sum(weight), (1, 2, rows))
    sums = jnp.concatenate([sums, count]).reshape(3, 2 * rows)
    sums = sums + lax.ppermute(sums, "c", PAIR)
    totals = spread(sums, ("zl", "zh"), 8)
    totals = jnp.sum(totals, 0)
    totals = totals.reshape(3, 2, rows)
    totals = jnp.where(core == 0, totals, totals[:, ::-1]).reshape(3, 2 * rows)
    bg_mean = totals[0] / totals[2]
    bg_std = jnp.sqrt(totals[1] / totals[2] - bg_mean * bg_mean + EPSILON)
    normed = ((whitened - bg_mean[:, None]) / bg_std[:, None]).astype(BF16)

    first, second = jnp.where(core == 0, x, y), jnp.where(core == 0, y, x)
    refs = put_together(jnp.stack([zl, core, first, second]), sheet)
    refs = refs.reshape(32 * views, half)
    ref_energy = jnp.sum(jnp.square(refs.astype(F32)), 1)
    score = lambda a: (
        lax.dot_general(a, refs, (((1,), (1,)), ((), ())), preferred_element_type=F32)
        - 0.5 * ref_energy[None, :]
    )
    both = lax.ppermute(score(normed[rows:]), "c", PAIR)
    both = both + lax.optimization_barrier(score(normed[:rows]))
    both = both.reshape(2, rows // 2, 32 * views)
    cut = 16 * views
    kept = lax.dynamic_index_in_dim(both, zl, 0, False)
    sent = lax.dynamic_index_in_dim(both, 1 - zl, 0, False)
    kept = kept + jnp.concatenate([swap(sent[:, :cut]), far(sent[:, cut:])], 1)
    up = lambda a: lax.ppermute(a, "zh", [(i, (i + 1) % 4) for i in range(4)])
    down = lambda a: lax.ppermute(a, "zh", [((i + 1) % 4, i) for i in range(4)])
    take = lambda step, skip, count: lax.dynamic_slice_in_dim(
        kept, (zh + step) % 4 * 32 + skip, count
    )
    pass_up, pass_down = lax.optimization_barrier((take(2, 0, 16), take(2, 16, 16)))
    came_up, came_down = lax.optimization_barrier((up(pass_up), down(pass_down)))
    to_next = jnp.concatenate([take(1, 0, 16) + came_up, take(1, 16, 16)])
    to_last = jnp.concatenate([take(3, 0, 16), take(3, 16, 16) + came_down])
    to_next, to_last = lax.optimization_barrier((to_next, to_last))
    came_up, came_down = lax.optimization_barrier((up(to_next), down(to_last)))
    scores = (take(0, 0, 32) + came_up + came_down) * (4.0 / SIDE)

    row_max = jnp.max(scores, 1, keepdims=True)
    log_total = row_max[:, 0] + jnp.log(jnp.sum(jnp.exp(scores - row_max), 1))
    evidence = log_total - jnp.mean(scores, 1)
    posterior = jnp.exp(scores - log_total[:, None]).astype(BF16)

    strip = spread(posterior, "zh", 4).reshape(rows // 2, -1)
    class_mass = jnp.sum(strip, 0, dtype=F32)
    onehot = (view_class[:, None] == jnp.arange(NCLS, dtype=jnp.int32)[None, :]).astype(F32)
    share = jnp.dot(class_mass[None], onehot, precision=lax.Precision.HIGHEST)
    share = spread(share, ("x", "y"), 16)
    share = jnp.sum(share, 0)
    other_strip = [swap(strip[:, :cut]), far(strip[:, cut:])]
    other_strip = jnp.concatenate(other_strip, 1)
    gathered = jnp.where(
        zl == 0, jnp.concatenate([strip, other_strip]), jnp.concatenate([other_strip, strip])
    )
    gathered_c = lax.ppermute(gathered, "c", PAIR)
    gathered = jnp.concatenate([gathered, gathered_c])
    share = share + swap(share)
    share = share + lax.ppermute(share, "c", PAIR)

    part = lax.dot_general(gathered, normed, (((0,), (0,)), ((), ())), preferred_element_type=F32)
    part = part.astype(BF16).reshape(32, views, half)
    part = lax.all_to_all(part, img, split_axis=0, concat_axis=0)
    part = jnp.sum(part.reshape(2, 16, views, half).astype(F32), 1)
    view_sums = jnp.concatenate([part[0], part[1]], 1)
    return (view_sums, share[0] * (NCLS / total_images), evidence)


def solution(mesh):
    fine = Mesh(mesh.devices.reshape(2, 4, 4, 4, 2), ("zl", "x", "y", "zh", "c"))
    img, pix = ("zl", "x", "y"), ("zh", "c")
    in_specs = (P(img, pix), P(img, pix), P(pix), P())
    out_specs = (P(img, pix), P(), P(img + pix))

    return jax.shard_map(
        on_device, mesh=fine, in_specs=in_specs, out_specs=out_specs, check_vma=False
    )
```

```python
import jax
import jax.numpy as jnp
from jax import lax
from jax.experimental import pallas as pl
from jax.experimental.pallas import tpu as pltpu
from jax.sharding import Mesh, PartitionSpec as P

SIDE = 128
NCLS = 96
EPSILON = 1e-05
BF16, F32 = jnp.bfloat16, jnp.float32
PAIR = [(0, 1), (1, 0)]
FAR = [(zh, 4 + (zh - 1) % 4) for zh in range(4)] + [(4 + zh, (zh + 1) % 4) for zh in range(4)]


def plane(step, first):
    pairs = []
    for x in range(4):
        for y in range(4):
            for core in range(2):
                along_x = (core == 0) == first
                to = ((x - step) % 4, y) if along_x else (x, (y - step) % 4)
                pairs.append((x * 8 + y * 2 + core, to[0] * 8 + to[1] * 2 + core))
    return pairs


def put_kernel(at, *refs):
    out, energy = refs[4], refs[5]
    zl, core, first, second = at[0], at[1], at[2], at[3]
    rows = out.shape[1]
    for t in range(4):
        q = (second + t) % 4
        for s in range(4):
            p = (first + s) % 4
            spot = jnp.where(core == 0, p * 4 + q, q * 4 + p)
            for k in range(2):
                piece = refs[t][s, k * rows : (k + 1) * rows]
                index = (zl + k) % 2 * 16 + spot
                out[index] = piece
                square = jnp.square(piece.astype(F32))
                energy[index] = sum(
                    square[:, lane : lane + 128] for lane in range(0, square.shape[1], 128)
                )


def put_together(at, parts):
    vmem = pl.BlockSpec(memory_space=pltpu.VMEM)
    rows, pixels = parts[0].shape[1] // 2, parts[0].shape[2]
    return pl.pallas_call(
        put_kernel,
        in_specs=[pl.BlockSpec(memory_space=pltpu.SMEM)] + [vmem] * 4,
        out_specs=(vmem, vmem),
        out_shape=(
            jax.ShapeDtypeStruct((32, rows, pixels), parts[0].dtype),
            jax.ShapeDtypeStruct((32, rows, 128), F32),
        ),
    )(at, *parts)


def spread(value, axes, count):
    sent = jnp.broadcast_to(value[None], (count,) + value.shape)
    return lax.all_to_all(sent, axes, split_axis=0, concat_axis=0)


def on_device(images, references, cycle_mask, view_class):
    zl, x, y, zh, core = (lax.axis_index(a) for a in ("zl", "x", "y", "zh", "c"))
    rows, wide = images.shape
    half = wide // 2
    views = references.shape[0]
    total_images = rows * 32
    img = ("zl", "x", "y")
    mine = lambda a, axis: lax.dynamic_slice_in_dim(a, zl * half, half, axis)
    theirs = lambda a, axis: lax.dynamic_slice_in_dim(a, (1 - zl) * half, half, axis)
    swap = lambda a: lax.ppermute(a, "zl", PAIR)
    far = lambda a: lax.ppermute(a, ("zl", "zh"), FAR)

    widened = images.astype(F32)
    local = jnp.stack([jnp.sum(widened, 0), jnp.sum(widened * widened, 0)])
    moments = swap(theirs(local, 1))
    moments = mine(local, 1) + moments
    plan = ("x", "y", "c")
    ref_other = swap(theirs(references, 1))
    ref_pair = jnp.concatenate([mine(references, 1), ref_other])
    line = [lax.ppermute(ref_pair, plan, plane(s, True)) for s in (1, 2, 3)]
    img_other = swap(theirs(images, 1))
    img_own = mine(images, 1)
    moments = spread(moments, ("x", "y"), 16)
    moments = jnp.sum(moments, 0)

    line = jnp.stack([ref_pair] + line)
    sheet = [line] + [lax.ppermute(line, plan, plane(s, False)) for s in (1, 2, 3)]

    shape = (4, 2, 32, half)
    own, other = img_own.reshape(shape), img_other.reshape(shape)
    pair = jnp.where(zl == 0, jnp.stack([own, other]), jnp.stack([other, own]))
    even, odd = pair[:, :, 0], pair[:, :, 1]
    block = jnp.where(core == 0, jnp.stack([even, odd]), jnp.stack([odd, even]))
    block = block.reshape(2 * rows, half)

    pix_mean = moments[0] / total_images
    pix_std = jnp.sqrt(moments[1] / total_images - pix_mean * pix_mean + EPSILON)
    whitened = (block.astype(F32) - pix_mean) / pix_std
    weight = mine(cycle_mask, 0).astype(F32)
    sums = jnp.stack([jnp.sum(whitened * weight, 1), jnp.sum(whitened * whitened * weight, 1)])
    sums = sums.reshape(2, 2, rows)
    sums = jnp.where(core == 0, sums, sums[:, ::-1])
    count = jnp.broadcast_to(jnp.sum(weight), (1, 2, rows))
    sums = jnp.concatenate([sums, count]).reshape(3, 2 * rows)
    sums = sums + lax.ppermute(sums, "c", PAIR)
    totals = spread(sums, ("zl", "zh"), 8)
    totals = jnp.sum(totals, 0)
    totals = totals.reshape(3, 2, rows)
    totals = jnp.where(core == 0, totals, totals[:, ::-1]).reshape(3, 2 * rows)
    bg_mean = totals[0] / totals[2]
    bg_std = jnp.sqrt(totals[1] / totals[2] - bg_mean * bg_mean + EPSILON)
    normed = ((whitened - bg_mean[:, None]) / bg_std[:, None]).astype(BF16)

    first, second = jnp.where(core == 0, x, y), jnp.where(core == 0, y, x)
    refs, energy = put_together(jnp.stack([zl, core, first, second]), sheet)
    refs = refs.reshape(32 * views, half)
    ref_energy = jnp.sum(energy, 2).reshape(-1)
    score = lambda a: (
        lax.dot_general(a, refs, (((1,), (1,)), ((), ())), preferred_element_type=F32)
        - 0.5 * ref_energy[None, :]
    )
    theirs_part = lax.ppermute(score(normed[rows:]), "c", PAIR)
    own_part = lax.optimization_barrier(score(normed[:rows]))
    cut = 16 * views
    deep = rows // 2

    def added(place, start, count):
        at, size = (place * deep, start), (deep, count)
        return lax.dynamic_slice(theirs_part, at, size) + lax.dynamic_slice(own_part, at, size)

    leaving = lax.optimization_barrier((added(1 - zl, 0, cut), added(1 - zl, cut, cut)))
    came = jnp.concatenate([swap(leaving[0]), far(leaving[1])], 1)
    kept = added(zl, 0, 2 * cut) + came
    up = lambda a: lax.ppermute(a, "zh", [(i, (i + 1) % 4) for i in range(4)])
    down = lambda a: lax.ppermute(a, "zh", [((i + 1) % 4, i) for i in range(4)])
    take = lambda step, skip, count: lax.dynamic_slice_in_dim(
        kept, (zh + step) % 4 * 32 + skip, count
    )
    pass_up, pass_down = lax.optimization_barrier((take(2, 0, 16), take(2, 16, 16)))
    came_up, came_down = lax.optimization_barrier((up(pass_up), down(pass_down)))
    to_next = jnp.concatenate([take(1, 0, 16) + came_up, take(1, 16, 16)])
    to_last = jnp.concatenate([take(3, 0, 16), take(3, 16, 16) + came_down])
    to_next, to_last = lax.optimization_barrier((to_next, to_last))
    came_up, came_down = lax.optimization_barrier((up(to_next), down(to_last)))
    scores = (take(0, 0, 32) + came_up + came_down) * (4.0 / SIDE)

    row_max = jnp.max(scores, 1, keepdims=True)
    log_total = row_max[:, 0] + jnp.log(jnp.sum(jnp.exp(scores - row_max), 1))
    evidence = log_total - jnp.mean(scores, 1)
    posterior = jnp.exp(scores - log_total[:, None]).astype(BF16)

    strip = spread(posterior, "zh", 4).reshape(rows // 2, -1)
    class_mass = jnp.sum(strip, 0, dtype=F32)
    onehot = (view_class[:, None] == jnp.arange(NCLS, dtype=jnp.int32)[None, :]).astype(F32)
    share = jnp.dot(class_mass[None], onehot, precision=lax.Precision.HIGHEST)
    share = spread(share, ("x", "y"), 16)
    share = jnp.sum(share, 0)
    other_strip = [swap(strip[:, :cut]), far(strip[:, cut:])]
    other_strip = jnp.concatenate(other_strip, 1)
    gathered = jnp.where(
        zl == 0, jnp.concatenate([strip, other_strip]), jnp.concatenate([other_strip, strip])
    )
    gathered_c = lax.ppermute(gathered, "c", PAIR)
    gathered = jnp.concatenate([gathered, gathered_c])
    share = share + swap(share)
    share = share + lax.ppermute(share, "c", PAIR)

    part = lax.dot_general(gathered, normed, (((0,), (0,)), ((), ())), preferred_element_type=F32)
    part = part.astype(BF16).reshape(32, views, half)
    part = lax.all_to_all(part, img, split_axis=0, concat_axis=0)
    part = jnp.sum(part.reshape(2, 16, views, half).astype(F32), 1)
    view_sums = jnp.concatenate([part[0], part[1]], 1)
    return (view_sums, share[0] * (NCLS / total_images), evidence)


def solution(mesh):
    fine = Mesh(mesh.devices.reshape(2, 4, 4, 4, 2), ("zl", "x", "y", "zh", "c"))
    img, pix = ("zl", "x", "y"), ("zh", "c")
    in_specs = (P(img, pix), P(img, pix), P(pix), P())
    out_specs = (P(img, pix), P(), P(img + pix))

    return jax.shard_map(
        on_device, mesh=fine, in_specs=in_specs, out_specs=out_specs, check_vma=False
    )
```
